128 devices in a mesh: tok: 8 (over y, core), hid: 16 (over z, x).
Axes of the slice: x: 4, y: 4, z: 4, core: 2. Of those that a mesh axis runs over, the one named last changes fastest.
Arguments:
- tokens: float32 [2048, 4096], P('tok', 'hid'), may hold values from -6 to 6
- upstream: float32 [2048, 4096], P('tok', 'hid'), may hold values from -6 to 6
- relu_mask: int32 [2048, 14336], P('tok', 'hid'), may hold values 0 or 1
- weight_in: float32 [1344, 128, 128], P('hid'), may hold values from -0.1875 to 0.1875
- weight_out: float32 [1344, 128, 128], P('hid'), may hold values from -0.09375 to 0.09375
- kept_in: int32 [1344, 2], P('hid'), may hold values from 0 to 31, as said below
- kept_out: int32 [1344, 2], P('hid'), may hold values from 0 to 31, as said below
- kept_count: int32 [16, 2], P('hid'), may hold values from 42 to 84, as said below
Outputs:
- token_grad: float32 [2048, 4096], P('tok', 'hid')
- grad_in: float32 [1344, 128, 128], P('hid', 'tok')
- grad_out: float32 [1344, 128, 128], P('hid', 'tok')
The draws below stay inside these ranges and needn't reach their ends.
Inputs may be any that keep to these rules, and one draw needn't show every extreme that they name: `kept_in`: row j * 84 + s belongs to hidden shard j. Its first entry is a block row of the model width, its second a hidden block of that shard (0 to 6). The live slots of one shard name distinct blocks, and their block rows are among ((j - 1) * 2 + m) mod 32 for m from 0 to 19; slots that are not live hold 0 and 0. `kept_out`: row j * 84 + s belongs to hidden shard j. Its first entry is a hidden block of that shard (0 to 6), its second a block column of the model width. The live slots of one shard name distinct blocks, and their block columns are among ((j - 1) * 2 + m) mod 32 for m from 0 to 19; slots that are not live hold 0 and 0. kept_count[j, 0] and kept_count[j, 1] are the live slots of shard j in weight_in and weight_out; for each of the two some shard has exactly 84.
All inputs are finite; a program needn't handle non-finite values. No bound on the sum of `relu_mask` on one device may be relied on, other than what follows from the above.
Results may differ from the reference program's by a relative error of at most 0.0003.
Values sent between devices are 32-bit elements; how exact they have to be, the bound alone decides.
No kernel may reach another device: no remote copies, remote signals or barrier semaphores. Data moves between devices by JAX's collectives and lax.ppermute only.
A program may use at most 192 MiB of HBM per device.

```python
import math
import jax
import jax.numpy as jnp
from jax import lax

D = 4096
FF = 14336
BLK = 128
TOKENS = 2048
DB = 32
HB_DEV = 7
CAP = 84
WIN = 20
N_HID = 16


def block_lists(key, which):
    key = jax.random.fold_in(key, 7001 + which)
    key_count, key_heavy, key_score = jax.random.split(key, 3)
    counts = jax.random.randint(key_count, (N_HID,), CAP // 2, CAP + 1)
    heavy = jax.random.randint(key_heavy, (), 0, N_HID)
    counts = jnp.where(jnp.arange(N_HID, dtype=jnp.int32) == heavy, CAP, counts).astype(jnp.int32)
    centers = (jnp.arange(N_HID, dtype=jnp.int32) - 1) * (DB // N_HID) % DB
    pair_index = jnp.arange(DB * HB_DEV, dtype=jnp.int32)
    width_block = pair_index // HB_DEV
    hidden_block = pair_index % HB_DEV
    distance = (width_block[None, :] - centers[:, None]) % DB
    inside = (distance < WIN).astype(jnp.int32)
    noise = jax.random.randint(key_score, (N_HID, DB * HB_DEV), 0, 4096)
    scores = inside * (1 << 24) + noise * 1024 + pair_index[None, :]
    _, chosen = lax.top_k(scores, CAP)
    live = jnp.arange(CAP, dtype=jnp.int32)[None, :] < counts[:, None]
    width_sel = jnp.where(live, width_block[chosen], 0)
    hidden_sel = jnp.where(live, hidden_block[chosen], 0)
    if which == 0:
        lists = jnp.stack([width_sel, hidden_sel], axis=-1)
    else:
        lists = jnp.stack([hidden_sel, width_sel], axis=-1)
    return (lists.reshape(N_HID * CAP, 2).astype(jnp.int32), counts)


def draw_kept_in(key, part):
    lists, counts = block_lists(key, 0)
    return lists


def draw_kept_out(key, part):
    lists, counts = block_lists(key, 1)
    return lists


def draw_kept_count(key, part):
    lists_first, counts_first = block_lists(key, 0)
    lists_second, counts_second = block_lists(key, 1)
    return jnp.stack([counts_first, counts_second], axis=-1).astype(jnp.int32)


def touch_ends(drawn, own_key, least, largest):
    index_at = [jax.random.randint(jax.random.fold_in(own_key, axis), (), 0, length) for axis, length in enumerate(drawn.shape)]
    main_axis = drawn.shape.index(max(drawn.shape))
    next_to = index_at[:main_axis] + [(index_at[main_axis] + 1) % drawn.shape[main_axis]] + index_at[main_axis + 1:]
    return drawn.at[tuple(index_at)].set(least).at[tuple(next_to)].set(largest)


def steps_of(own_key, shape, cuts, least, high):
    loudness, own = 1.0, jax.random.fold_in(own_key, 6)
    for position, blocks in cuts:
        draws = jnp.exp(jax.random.uniform(jax.random.fold_in(own, position), (blocks,), jnp.float32, least / len(cuts), high / len(cuts)))
        loudness = loudness * jnp.repeat(draws, shape[position] // blocks).reshape([-1 if axis == position else 1 for axis in range(len(shape))])
    return loudness


def normal_values(rng, shape, deviation, limit, cuts=(), kind=jnp.bfloat16):
    loudness = steps_of(rng, shape, cuts, -0.22, 0.18) if cuts else 1.0
    result = jax.random.normal(rng, shape, jnp.float32) * deviation * loudness
    return jnp.minimum(jnp.maximum(result, -limit), limit).astype(kind)


def setup_inputs(seed: int = 0) -> dict:
    streams_of = jax.random.split(jax.random.key(seed), 9)
    tokens = normal_values(streams_of[0], (TOKENS, D), 1.0, 6.0, ((0, 8), (1, 16)), jnp.float32)
    upstream = normal_values(streams_of[1], (TOKENS, D), 1.0, 6.0, ((0, 8), (1, 16)), jnp.float32)
    relu_mask = touch_ends((jax.random.randint(streams_of[2], (TOKENS, FF), 0, 2) < 1).astype(jnp.int32), jax.random.fold_in(streams_of[2], 1), 0, 1)
    weight_in = normal_values(streams_of[3], (N_HID * CAP, BLK, BLK), (D // 4) ** -0.5, 0.1875, ((0, 16),), jnp.float32)
    weight_out = normal_values(streams_of[4], (N_HID * CAP, BLK, BLK), (FF // 4) ** -0.5, 0.09375, ((0, 16),), jnp.float32)
    kept_in = draw_kept_in(jax.random.fold_in(streams_of[8], 71), 0)
    kept_out = draw_kept_out(jax.random.fold_in(streams_of[8], 71), 0)
    kept_count = draw_kept_count(jax.random.fold_in(streams_of[8], 71), 0)
    return dict(tokens=tokens, upstream=upstream, relu_mask=relu_mask, weight_in=weight_in, weight_out=weight_out, kept_in=kept_in, kept_out=kept_out, kept_count=kept_count)


HIGH = lax.Precision.HIGHEST

def local_pass(token_blocks, upstream_blocks, active, weight_in, weight_out, kept_in, kept_out, count_in, count_out):
    block_count = token_blocks.shape[1]
    hidden_count = active.shape[1]
    slots = jnp.arange(weight_in.shape[0], dtype=jnp.int32)
    live_in = (slots < count_in).astype(jnp.float32)
    live_out = (slots < count_out).astype(jnp.float32)
    weight_in_live = weight_in * live_in[:, None, None]
    weight_out_live = weight_out * live_out[:, None, None]
    pick_in = (kept_in[:, 1][:, None] == jnp.arange(hidden_count, dtype=jnp.int32)[None, :]).astype(jnp.float32)
    rows_in = (kept_in[:, 0][:, None] == jnp.arange(block_count, dtype=jnp.int32)[None, :]).astype(jnp.float32)
    pick_out = (kept_out[:, 0][:, None] == jnp.arange(hidden_count, dtype=jnp.int32)[None, :]).astype(jnp.float32)
    token_sel = jnp.take(token_blocks, kept_in[:, 0], axis=1)
    product = jnp.einsum('tsk,skn->tsn', token_sel, weight_in_live, precision=HIGH)
    pre = jnp.einsum('tsn,sh->thn', product, pick_in, precision=HIGH)
    hidden = pre * active
    upstream_sel = jnp.take(upstream_blocks, kept_out[:, 1], axis=1)
    back = jnp.einsum('tsn,skn->tsk', upstream_sel, weight_out_live, precision=HIGH)
    back = jnp.einsum('tsk,sh->thk', back, pick_out, precision=HIGH)
    dhidden = back * active
    dhidden_sel = jnp.take(dhidden, kept_in[:, 1], axis=1)
    terms = jnp.einsum('tsn,skn->tsk', dhidden_sel, weight_in_live, precision=HIGH)
    terms = jnp.einsum('tsk,sr->trk', terms, rows_in, precision=HIGH)
    grad_in = jnp.einsum('tsk,tsn->skn', token_sel, dhidden_sel, precision=HIGH) * live_in[:, None, None]
    hidden_sel = jnp.take(hidden, kept_out[:, 0], axis=1)
    grad_out = jnp.einsum('tsk,tsn->skn', hidden_sel, upstream_sel, precision=HIGH) * live_out[:, None, None]
    return (terms, grad_in, grad_out)

def reference(tokens, upstream, relu_mask, weight_in, weight_out, kept_in, kept_out, kept_count):
    token_blocks = tokens.reshape(TOKENS, DB, BLK)
    upstream_blocks = upstream.reshape(TOKENS, DB, BLK)
    active_all = jnp.transpose(relu_mask.reshape(TOKENS, N_HID, HB_DEV, BLK), (1, 0, 2, 3))
    scale = 1.0 / math.sqrt(TOKENS)

    def one_shard(total, inputs):
        active, w_first, w_second, k_first, k_second, counts = inputs
        terms, g_first, g_second = local_pass(token_blocks, upstream_blocks, active.astype(jnp.float32), w_first, w_second, k_first, k_second, counts[0], counts[1])
        return (total + terms, (g_first * scale, g_second * scale))
    start = jnp.zeros((TOKENS, DB, BLK), jnp.float32)
    inputs = (active_all, weight_in.reshape(N_HID, CAP, BLK, BLK), weight_out.reshape(N_HID, CAP, BLK, BLK), kept_in.reshape(N_HID, CAP, 2), kept_out.reshape(N_HID, CAP, 2), kept_count)
    total, grads = lax.scan(one_shard, start, inputs)
    grad_in = grads[0].reshape(N_HID * CAP, BLK, BLK)
    grad_out = grads[1].reshape(N_HID * CAP, BLK, BLK)
    return (total.reshape(TOKENS, D), grad_in, grad_out)
```

```python
import math

import jax
import jax.numpy as jnp
from jax import lax
from jax.experimental import pallas as pl
from jax.experimental.pallas import tpu as pltpu
from jax.sharding import PartitionSpec as P

DB = 32
BLK = 128
SLOTS_A_STEP = 12

F32 = jnp.float32
BF16 = jnp.bfloat16


def halves(x):
    hi = x.astype(BF16)
    lo = (x - hi.astype(F32)).astype(BF16)
    return hi, lo


def dot_nn(a, b):
    return lax.dot_general(a, b, (((1,), (0,)), ((), ())), preferred_element_type=F32)


def dot_nt(a, b):
    return lax.dot_general(a, b, (((1,), (1,)), ((), ())), preferred_element_type=F32)


def params(mib):
    return pltpu.CompilerParams(
        dimension_semantics=("arbitrary",), vmem_limit_bytes=mib * 1024 * 1024
    )


def dense_in_kernel(m_ref, h_ref, n_ref, w_ref, hi_ref, lo_ref):
    step = pl.program_id(0)

    @pl.when(step == 0)
    def _():
        hi_ref[...] = jnp.zeros_like(hi_ref)
        lo_ref[...] = jnp.zeros_like(lo_ref)

    for q in range(SLOTS_A_STEP):
        s = step * SLOTS_A_STEP + q

        @pl.when(s < n_ref[0])
        def _():
            hi, lo = halves(w_ref[q])
            col = pl.multiple_of(h_ref[s] * BLK, BLK)
            hi_ref[m_ref[s], :, pl.ds(col, BLK)] = hi
            lo_ref[m_ref[s], :, pl.ds(col, BLK)] = lo


def dense_out_kernel(m_ref, h_ref, n_ref, w_ref, hi_ref, lo_ref):
    step = pl.program_id(0)

    @pl.when(step == 0)
    def _():
        hi_ref[...] = jnp.zeros_like(hi_ref)
        lo_ref[...] = jnp.zeros_like(lo_ref)

    for q in range(SLOTS_A_STEP):
        s = step * SLOTS_A_STEP + q

        @pl.when(s < n_ref[0])
        def _():
            hi, lo = halves(w_ref[q])
            row = pl.multiple_of(h_ref[s] * BLK, BLK)
            col = pl.multiple_of((m_ref[s] % 2) * BLK, BLK)
            hi_ref[m_ref[s] // 2, pl.ds(row, BLK), pl.ds(col, BLK)] = hi
            lo_ref[m_ref[s] // 2, pl.ds(row, BLK), pl.ds(col, BLK)] = lo


def dense(kernel, weight, place, hidden, count, shape):
    slots = weight.shape[0]
    out = jax.ShapeDtypeStruct(shape, BF16)
    whole = pl.BlockSpec(shape, lambda i, *_: (0, 0, 0))
    return pl.pallas_call(
        kernel,
        out_shape=(out, out),
        grid_spec=pltpu.PrefetchScalarGridSpec(
            num_scalar_prefetch=3,
            grid=(slots // SLOTS_A_STEP,),
            in_specs=[pl.BlockSpec((SLOTS_A_STEP, BLK, BLK), lambda i, *_: (i, 0, 0))],
            out_specs=(whole, whole),
        ),
        compiler_params=params(48),
    )(place, hidden, count, weight)


def back_kernel(j_ref, u_ref, whi_ref, wlo_ref, mask_ref, uc_ref, dhi_ref, dlo_ref, dh_ref, acc):
    step = pl.program_id(0)
    hi, lo = halves(u_ref[0])
    part = dot_nt(hi, whi_ref[0]) + dot_nt(hi, wlo_ref[0]) + dot_nt(lo, whi_ref[0])

    @pl.when(step == 0)
    def _():
        acc[...] = part

    @pl.when(step > 0)
    def _():
        acc[...] += part

    for b in range(2):
        uc_ref[b, :, :BLK] = hi[:, b * BLK : (b + 1) * BLK]
        uc_ref[b, :, BLK:] = lo[:, b * BLK : (b + 1) * BLK]

    @pl.when(step == pl.num_programs(0) - 1)
    def _():
        d = acc[...] * mask_ref[...].astype(F32)
        dhi, dlo = halves(d)
        dhi_ref[...] = dhi
        dlo_ref[...] = dlo
        for h in range(dh_ref.shape[0]):
            dh_ref[h, :, :BLK] = dhi[:, h * BLK : (h + 1) * BLK]
            dh_ref[h, :, BLK:] = dlo[:, h * BLK : (h + 1) * BLK]


def terms_kernel(dhi_ref, dlo_ref, whi_ref, wlo_ref, out_ref):
    hidden = dhi_ref.shape[1]
    whi = whi_ref[...].reshape(2 * BLK, hidden)
    wlo = wlo_ref[...].reshape(2 * BLK, hidden)
    hi = dhi_ref[...]
    out_ref[0] = dot_nt(hi, whi) + dot_nt(hi, wlo) + dot_nt(dlo_ref[...], whi)


def pre_kernel(j_ref, t_ref, whi_ref, wlo_ref, mask_ref, tt_ref, ht_ref, acc):
    step = pl.program_id(0)
    hidden = acc.shape[1]
    t = t_ref[0]
    hi, lo = halves(t)
    whi = whi_ref[...].reshape(2 * BLK, hidden)
    wlo = wlo_ref[...].reshape(2 * BLK, hidden)
    part = dot_nn(hi, whi) + dot_nn(hi, wlo) + dot_nn(lo, whi)

    @pl.when(step == 0)
    def _():
        acc[...] = part

    @pl.when(step > 0)
    def _():
        acc[...] += part

    for b in range(2):
        thi, tlo = halves(t[:, b * BLK : (b + 1) * BLK].T)
        tt_ref[b, :BLK, :] = thi
        tt_ref[b, BLK:, :] = tlo

    @pl.when(step == pl.num_programs(0) - 1)
    def _():
        hid = acc[...] * mask_ref[...].astype(F32)
        for h in range(ht_ref.shape[0]):
            hhi, hlo = halves(hid[:, h * BLK : (h + 1) * BLK].T)
            ht_ref[h, :BLK, :] = hhi
            ht_ref[h, BLK:, :] = hlo


def grad_kernel(scale, a_ref, b_ref, n_ref, left_ref, right_ref, out_ref):
    step = pl.program_id(0)
    rows = out_ref.shape[2]
    for q in range(SLOTS_A_STEP):
        s = step * SLOTS_A_STEP + q

        @pl.when(s < n_ref[0])
        def _():
            r = dot_nn(left_ref[a_ref[s]], right_ref[b_ref[s]])
            g = (r[:BLK, :BLK] + (r[:BLK, BLK:] + r[BLK:, :BLK] + r[BLK:, BLK:])) * scale
            out_ref[:, q] = g.reshape(BLK // rows, rows, BLK)

        @pl.when(s >= n_ref[0])
        def _():
            out_ref[:, q] = jnp.zeros((BLK // rows, rows, BLK), F32)


def grads(left, right, a, b, count, slots, peers, scale):
    rows = BLK // peers
    return pl.pallas_call(
        lambda *refs: grad_kernel(scale, *refs),
        out_shape=jax.ShapeDtypeStruct((peers, slots, rows, BLK), F32),
        grid_spec=pltpu.PrefetchScalarGridSpec(
            num_scalar_prefetch=3,
            grid=(slots // SLOTS_A_STEP,),
            in_specs=[
                pl.BlockSpec(left.shape, lambda i, *_: (0, 0, 0)),
                pl.BlockSpec(right.shape, lambda i, *_: (0, 0, 0)),
            ],
            out_specs=pl.BlockSpec((peers, SLOTS_A_STEP, rows, BLK), lambda i, *_: (0, i, 0, 0)),
        ),
        compiler_params=params(40),
    )(a, b, count, left, right)


def sum_over_tok(value):
    peers, slots, rows, width = value.shape
    flat = value.reshape(peers * slots * rows, width)
    return lax.psum_scatter(flat, "tok", scatter_dimension=0, tiled=True).reshape(
        slots, rows, width
    )


def per_device(tokens, upstream, relu_mask, weight_in, weight_out, kept_in, kept_out, kept_count):
    peers = lax.axis_size("hid")
    tok_peers = lax.axis_size("tok")
    j = lax.axis_index("hid").astype(jnp.int32)
    rows, width = tokens.shape
    hidden = relu_mask.shape[1]
    hidden_count = hidden // BLK
    slots = weight_in.shape[0]
    per_shard = width // BLK
    sources = 10
    band = sources * per_shard
    scale = 1.0 / math.sqrt(rows * tok_peers)
    first = (j - 1) * per_shard
    m_in = (kept_in[:, 0] - first) % DB
    m_in = jnp.where(m_in < band, m_in, 0)
    h_in = jnp.clip(kept_in[:, 1], 0, hidden_count - 1)
    h_out = jnp.clip(kept_out[:, 0], 0, hidden_count - 1)
    m_out = (kept_out[:, 1] - first) % DB
    m_out = jnp.where(m_out < band, m_out, 0)
    n_in = kept_count[0, 0].reshape(1)
    n_out = kept_count[0, 1].reshape(1)

    up = lax.all_gather(upstream, "hid", axis=0, tiled=True).reshape(peers, rows, width)
    tk = lax.all_gather(tokens, "hid", axis=0, tiled=True).reshape(peers, rows, width)

    w2hi, w2lo = dense(dense_out_kernel, weight_out, m_out, h_out, n_out, (sources, hidden, width))
    w1hi, w1lo = dense(dense_in_kernel, weight_in, m_in, h_in, n_in, (band, BLK, hidden))

    shard = pl.BlockSpec((1, rows, width), lambda i, jr: ((jr[0] + i + peers - 1) % peers, 0, 0))
    whole_mask = pl.BlockSpec((rows, hidden), lambda i, jr: (0, 0))
    pairs = pl.BlockSpec((per_shard, rows, width), lambda i, jr: (i, 0, 0))
    per_hidden = pl.BlockSpec((hidden_count, rows, width), lambda i, jr: (0, 0, 0))
    flat_hidden = pl.BlockSpec((rows, hidden), lambda i, jr: (0, 0))
    uc, dhi, dlo, dh = pl.pallas_call(
        back_kernel,
        out_shape=(
            jax.ShapeDtypeStruct((band, rows, width), BF16),
            jax.ShapeDtypeStruct((rows, hidden), BF16),
            jax.ShapeDtypeStruct((rows, hidden), BF16),
            jax.ShapeDtypeStruct((hidden_count, rows, width), BF16),
        ),
        grid_spec=pltpu.PrefetchScalarGridSpec(
            num_scalar_prefetch=1,
            grid=(sources,),
            in_specs=[
                shard,
                pl.BlockSpec((1, hidden, width), lambda i, jr: (i, 0, 0)),
                pl.BlockSpec((1, hidden, width), lambda i, jr: (i, 0, 0)),
                whole_mask,
            ],
            out_specs=(pairs, flat_hidden, flat_hidden, per_hidden),
            scratch_shapes=[pltpu.VMEM((rows, hidden), F32)],
        ),
        compiler_params=params(40),
    )(j.reshape(1), up, w2hi, w2lo, relu_mask)

    terms = pl.pallas_call(
        terms_kernel,
        out_shape=jax.ShapeDtypeStruct((sources, rows, width), F32),
        grid=(sources,),
        in_specs=[
            pl.BlockSpec((rows, hidden), lambda i: (0, 0)),
            pl.BlockSpec((rows, hidden), lambda i: (0, 0)),
            pl.BlockSpec((per_shard, BLK, hidden), lambda i: (i, 0, 0)),
            pl.BlockSpec((per_shard, BLK, hidden), lambda i: (i, 0, 0)),
        ],
        out_specs=pl.BlockSpec((1, rows, width), lambda i: (i, 0, 0)),
        compiler_params=params(40),
    )(dhi, dlo, w1hi, w1lo)

    tt, ht = pl.pallas_call(
        pre_kernel,
        out_shape=(
            jax.ShapeDtypeStruct((band, rows, width), BF16),
            jax.ShapeDtypeStruct((hidden_count, rows, width), BF16),
        ),
        grid_spec=pltpu.PrefetchScalarGridSpec(
            num_scalar_prefetch=1,
            grid=(sources,),
            in_specs=[
                shard,
                pl.BlockSpec((per_shard, BLK, hidden), lambda i, jr: (i, 0, 0)),
                pl.BlockSpec((per_shard, BLK, hidden), lambda i, jr: (i, 0, 0)),
                whole_mask,
            ],
            out_specs=(pairs, per_hidden),
            scratch_shapes=[pltpu.VMEM((rows, hidden), F32)],
        ),
        compiler_params=params(40),
    )(j.reshape(1), tk, w1hi, w1lo, relu_mask)

    g_in = grads(tt, dh, m_in, h_in, n_in, slots, tok_peers, scale)
    grad_in = sum_over_tok(g_in)
    g_out = grads(ht, uc, h_out, m_out, n_out, slots, tok_peers, scale)
    grad_out = sum_over_tok(g_out)

    token_grad = terms[1]
    for i in range(sources):
        if i != 1:
            pairs_i = [(s, (s - 1 + i) % peers) for s in range(peers)]
            token_grad = token_grad + lax.ppermute(terms[i], "hid", pairs_i)
    return (token_grad, grad_in, grad_out)


def solution(mesh):
    return jax.shard_map(
        per_device,
        mesh=mesh,
        in_specs=(
            P("tok", "hid"),
            P("tok", "hid"),
            P("tok", "hid"),
            P("hid", None, None),
            P("hid", None, None),
            P("hid", None),
            P("hid", None),
            P("hid", None),
        ),
        out_specs=(P("tok", "hid"), P("hid", "tok", None), P("hid", "tok", None)),
        check_vma=False,
    )
```

```python
import math

import jax
import jax.numpy as jnp
from jax import lax
from jax.experimental import pallas as pl
from jax.experimental.pallas import tpu as pltpu
from jax.sharding import PartitionSpec as P

DB = 32
BLK = 128
SLOTS_A_STEP = 12
SIDE = 4

F32 = jnp.float32
BF16 = jnp.bfloat16


def halves(x):
    hi = x.astype(BF16)
    lo = (x - hi.astype(F32)).astype(BF16)
    return hi, lo


def dot_nn(a, b):
    return lax.dot_general(a, b, (((1,), (0,)), ((), ())), preferred_element_type=F32)


def dot_nt(a, b):
    return lax.dot_general(a, b, (((1,), (1,)), ((), ())), preferred_element_type=F32)


def params(mib):
    return pltpu.CompilerParams(
        dimension_semantics=("arbitrary",), vmem_limit_bytes=mib * 1024 * 1024
    )


def dense_in_kernel(m_ref, h_ref, n_ref, w_ref, hi_ref, lo_ref):
    step = pl.program_id(0)

    @pl.when(step == 0)
    def _():
        hi_ref[...] = jnp.zeros_like(hi_ref)
        lo_ref[...] = jnp.zeros_like(lo_ref)

    for q in range(SLOTS_A_STEP):
        s = step * SLOTS_A_STEP + q

        @pl.when(s < n_ref[0])
        def _():
            hi, lo = halves(w_ref[q])
            col = pl.multiple_of(h_ref[s] * BLK, BLK)
            hi_ref[m_ref[s], :, pl.ds(col, BLK)] = hi
            lo_ref[m_ref[s], :, pl.ds(col, BLK)] = lo


def dense_out_kernel(m_ref, h_ref, n_ref, w_ref, hi_ref, lo_ref):
    step = pl.program_id(0)

    @pl.when(step == 0)
    def _():
        hi_ref[...] = jnp.zeros_like(hi_ref)
        lo_ref[...] = jnp.zeros_like(lo_ref)

    for q in range(SLOTS_A_STEP):
        s = step * SLOTS_A_STEP + q

        @pl.when(s < n_ref[0])
        def _():
            hi, lo = halves(w_ref[q])
            row = pl.multiple_of(h_ref[s] * BLK, BLK)
            col = pl.multiple_of((m_ref[s] % 2) * BLK, BLK)
            hi_ref[m_ref[s] // 2, pl.ds(row, BLK), pl.ds(col, BLK)] = hi
            lo_ref[m_ref[s] // 2, pl.ds(row, BLK), pl.ds(col, BLK)] = lo


def dense(kernel, weight, place, hidden, count, shape):
    slots = weight.shape[0]
    out = jax.ShapeDtypeStruct(shape, BF16)
    whole = pl.BlockSpec(shape, lambda i, *_: (0, 0, 0))
    return pl.pallas_call(
        kernel,
        out_shape=(out, out),
        grid_spec=pltpu.PrefetchScalarGridSpec(
            num_scalar_prefetch=3,
            grid=(slots // SLOTS_A_STEP,),
            in_specs=[pl.BlockSpec((SLOTS_A_STEP, BLK, BLK), lambda i, *_: (i, 0, 0))],
            out_specs=(whole, whole),
        ),
        compiler_params=params(48),
    )(place, hidden, count, weight)


def back_kernel(j_ref, u_ref, whi_ref, wlo_ref, mask_ref, uc_ref, dhi_ref, dlo_ref, dh_ref, acc):
    step = pl.program_id(0)
    hi, lo = halves(u_ref[0])
    part = dot_nt(hi, whi_ref[0]) + dot_nt(hi, wlo_ref[0]) + dot_nt(lo, whi_ref[0])

    @pl.when(step == 0)
    def _():
        acc[...] = part

    @pl.when(step > 0)
    def _():
        acc[...] += part

    for b in range(2):
        uc_ref[b, :, :BLK] = hi[:, b * BLK : (b + 1) * BLK]
        uc_ref[b, :, BLK:] = lo[:, b * BLK : (b + 1) * BLK]

    @pl.when(step == pl.num_programs(0) - 1)
    def _():
        d = acc[...] * mask_ref[...].astype(F32)
        dhi, dlo = halves(d)
        dhi_ref[...] = dhi
        dlo_ref[...] = dlo
        for h in range(dh_ref.shape[0]):
            dh_ref[h, :, :BLK] = dhi[:, h * BLK : (h + 1) * BLK]
            dh_ref[h, :, BLK:] = dlo[:, h * BLK : (h + 1) * BLK]


def terms_kernel(dhi_ref, dlo_ref, whi_ref, wlo_ref, out_ref):
    hidden = dhi_ref.shape[1]
    whi = whi_ref[...].reshape(2 * BLK, hidden)
    wlo = wlo_ref[...].reshape(2 * BLK, hidden)
    hi = dhi_ref[...]
    out_ref[0] = dot_nt(hi, whi) + dot_nt(hi, wlo) + dot_nt(dlo_ref[...], whi)


def pre_kernel(j_ref, t_ref, whi_ref, wlo_ref, mask_ref, tt_ref, ht_ref, acc):
    step = pl.program_id(0)
    hidden = acc.shape[1]
    t = t_ref[0]
    hi, lo = halves(t)
    whi = whi_ref[...].reshape(2 * BLK, hidden)
    wlo = wlo_ref[...].reshape(2 * BLK, hidden)
    part = dot_nn(hi, whi) + dot_nn(hi, wlo) + dot_nn(lo, whi)

    @pl.when(step == 0)
    def _():
        acc[...] = part

    @pl.when(step > 0)
    def _():
        acc[...] += part

    for b in range(2):
        thi, tlo = halves(t[:, b * BLK : (b + 1) * BLK].T)
        tt_ref[b, :BLK, :] = thi
        tt_ref[b, BLK:, :] = tlo

    @pl.when(step == pl.num_programs(0) - 1)
    def _():
        hid = acc[...] * mask_ref[...].astype(F32)
        for h in range(ht_ref.shape[0]):
            hhi, hlo = halves(hid[:, h * BLK : (h + 1) * BLK].T)
            ht_ref[h, :BLK, :] = hhi
            ht_ref[h, BLK:, :] = hlo


def grad_kernel(scale, a_ref, b_ref, n_ref, at_ref, left_ref, right_ref, mine_ref, other_ref, buf):
    step = pl.program_id(0)
    hops, _, rows, _ = mine_ref.shape
    for q in range(SLOTS_A_STEP):
        s = step * SLOTS_A_STEP + q
        r = dot_nn(left_ref[a_ref[s]], right_ref[b_ref[s]])
        g = (r[:BLK, :BLK] + (r[:BLK, BLK:] + r[BLK:, :BLK] + r[BLK:, BLK:])) * scale
        buf[q] = jnp.where(s < n_ref[0], g, 0.0)
        for k in range(hops):
            mine_ref[k, q] = buf[q, pl.ds(pl.multiple_of(at_ref[k], rows), rows), :]
            other_ref[k, q] = buf[q, pl.ds(pl.multiple_of(at_ref[hops + k], rows), rows), :]


def grads(left, right, a, b, count, at, slots, peers, scale):
    rows = BLK // peers
    hops = peers // 2
    out = jax.ShapeDtypeStruct((hops, slots, rows, BLK), F32)
    out_spec = pl.BlockSpec((hops, SLOTS_A_STEP, rows, BLK), lambda i, *_: (0, i, 0, 0))
    return pl.pallas_call(
        lambda *refs: grad_kernel(scale, *refs),
        out_shape=(out, out),
        grid_spec=pltpu.PrefetchScalarGridSpec(
            num_scalar_prefetch=4,
            grid=(slots // SLOTS_A_STEP,),
            in_specs=[
                pl.BlockSpec(left.shape, lambda i, *_: (0, 0, 0)),
                pl.BlockSpec(right.shape, lambda i, *_: (0, 0, 0)),
            ],
            out_specs=(out_spec, out_spec),
            scratch_shapes=[pltpu.VMEM((SLOTS_A_STEP, BLK, BLK), F32)],
        ),
        compiler_params=params(40),
    )(a, b, count, at, left, right)


def from_z(value, k, only_x=None):
    pairs = [
        ((z + k) % SIDE * SIDE + x, z * SIDE + x)
        for z in range(SIDE)
        for x in range(SIDE)
        if only_x is None or x == only_x
    ]
    return lax.ppermute(value, "hid", pairs)


def from_x(value, k):
    pairs = [
        (z * SIDE + (x + k) % SIDE, z * SIDE + x) for z in range(SIDE) for x in range(SIDE)
    ]
    return lax.ppermute(value, "hid", pairs)


def from_y(value, k):
    pairs = [((y + k) % SIDE * 2 + c, y * 2 + c) for y in range(SIDE) for c in range(2)]
    return lax.ppermute(value, "tok", pairs)


def from_core(value):
    return lax.ppermute(value, "tok", [(i, i ^ 1) for i in range(2 * SIDE)])


def pick(value, start, count):
    return lax.dynamic_slice_in_dim(value, start.astype(jnp.int32), count, 0)


def band_z_first(own, x):
    next1, next2, before = from_z(own, 1), from_z(own, 2), from_z(own, -1, SIDE - 1)
    column = jnp.stack([before, own, next1, next2])
    right = from_x(pick(column, 1 + (x == 0), 2), 1)
    left = from_x(pick(column, 1 - (x == SIDE - 1), 3), -1)
    far0 = from_x(jnp.where(x == 0, right[1], right[0]), 1)
    far1 = from_x(jnp.where(x == SIDE - 1, left[1], left[2]), -1)
    return jnp.stack(
        [left[0], own, right[0], far0, left[1], next1, right[1], far1, left[2], next2]
    )


def band_x_first(own, x):
    row = [own, from_x(own, 1), from_x(own, 2), from_x(own, -1)]
    above = from_z(jnp.stack(row), 1)
    below = from_z(jnp.stack(row[2:]), -1)
    relayed = from_z(below, -1)
    top = from_z(above[:2], 1)
    above2 = [top[0], top[1], relayed[0], relayed[1]]
    near, far = [], []
    for d in range(1, SIDE):
        wrap = x + d >= SIDE
        near.append(jnp.where(wrap, above[d], row[d]))
        far.append(jnp.where(wrap, above2[d], above[d]))
    before = jnp.where(x == 0, below[1], row[3])
    return jnp.stack([before, own, *near, above[0], *far, above2[0]])


def sum_over_tok(mine, other):
    part = mine + from_core(other)
    half = part.shape[1] // 2
    up = from_y(part[2, :half], -1)
    down = from_y(part[2, half:], 1)
    to_up = jnp.concatenate([part[1, :half] + up, part[1, half:]])
    to_down = jnp.concatenate([part[3, :half], part[3, half:] + down])
    return part[0] + from_y(to_up, -1) + from_y(to_down, 1)


def per_device(tokens, upstream, relu_mask, weight_in, weight_out, kept_in, kept_out, kept_count):
    peers = lax.axis_size("hid")
    tok_peers = lax.axis_size("tok")
    j = lax.axis_index("hid").astype(jnp.int32)
    rows, width = tokens.shape
    hidden = relu_mask.shape[1]
    hidden_count = hidden // BLK
    slots = weight_in.shape[0]
    per_shard = width // BLK
    sources = 10
    band = sources * per_shard
    scale = 1.0 / math.sqrt(rows * tok_peers)
    first = (j - 1) * per_shard
    m_in = (kept_in[:, 0] - first) % DB
    m_in = jnp.where(m_in < band, m_in, 0)
    h_in = jnp.clip(kept_in[:, 1], 0, hidden_count - 1)
    h_out = jnp.clip(kept_out[:, 0], 0, hidden_count - 1)
    m_out = (kept_out[:, 1] - first) % DB
    m_out = jnp.where(m_out < band, m_out, 0)
    n_in = kept_count[0, 0].reshape(1)
    n_out = kept_count[0, 1].reshape(1)

    x = j % SIDE
    up = band_z_first(upstream, x)
    tk = band_x_first(tokens, x)
    t = lax.axis_index("tok").astype(jnp.int32)
    hop = jnp.arange(SIDE, dtype=jnp.int32)
    column = (t // 2 + hop) % SIDE * 2
    at = jnp.concatenate([column + t % 2, column + 1 - t % 2]) * (BLK // tok_peers)

    w2hi, w2lo = dense(dense_out_kernel, weight_out, m_out, h_out, n_out, (sources, hidden, width))
    w1hi, w1lo = dense(dense_in_kernel, weight_in, m_in, h_in, n_in, (band, BLK, hidden))

    shard = pl.BlockSpec((1, rows, width), lambda i, jr: (i, 0, 0))
    whole_mask = pl.BlockSpec((rows, hidden), lambda i, jr: (0, 0))
    pairs = pl.BlockSpec((per_shard, rows, width), lambda i, jr: (i, 0, 0))
    per_hidden = pl.BlockSpec((hidden_count, rows, width), lambda i, jr: (0, 0, 0))
    flat_hidden = pl.BlockSpec((rows, hidden), lambda i, jr: (0, 0))
    uc, dhi, dlo, dh = pl.pallas_call(
        back_kernel,
        out_shape=(
            jax.ShapeDtypeStruct((band, rows, width), BF16),
            jax.ShapeDtypeStruct((rows, hidden), BF16),
            jax.ShapeDtypeStruct((rows, hidden), BF16),
            jax.ShapeDtypeStruct((hidden_count, rows, width), BF16),
        ),
        grid_spec=pltpu.PrefetchScalarGridSpec(
            num_scalar_prefetch=1,
            grid=(sources,),
            in_specs=[
                shard,
                pl.BlockSpec((1, hidden, width), lambda i, jr: (i, 0, 0)),
                pl.BlockSpec((1, hidden, width), lambda i, jr: (i, 0, 0)),
                whole_mask,
            ],
            out_specs=(pairs, flat_hidden, flat_hidden, per_hidden),
            scratch_shapes=[pltpu.VMEM((rows, hidden), F32)],
        ),
        compiler_params=params(40),
    )(j.reshape(1), up, w2hi, w2lo, relu_mask)

    terms = pl.pallas_call(
        terms_kernel,
        out_shape=jax.ShapeDtypeStruct((sources, rows, width), F32),
        grid=(sources,),
        in_specs=[
            pl.BlockSpec((rows, hidden), lambda i: (0, 0)),
            pl.BlockSpec((rows, hidden), lambda i: (0, 0)),
            pl.BlockSpec((per_shard, BLK, hidden), lambda i: (i, 0, 0)),
            pl.BlockSpec((per_shard, BLK, hidden), lambda i: (i, 0, 0)),
        ],
        out_specs=pl.BlockSpec((1, rows, width), lambda i: (i, 0, 0)),
        compiler_params=params(40),
    )(dhi, dlo, w1hi, w1lo)

    tt, ht = pl.pallas_call(
        pre_kernel,
        out_shape=(
            jax.ShapeDtypeStruct((band, rows, width), BF16),
            jax.ShapeDtypeStruct((hidden_count, rows, width), BF16),
        ),
        grid_spec=pltpu.PrefetchScalarGridSpec(
            num_scalar_prefetch=1,
            grid=(sources,),
            in_specs=[
                shard,
                pl.BlockSpec((per_shard, BLK, hidden), lambda i, jr: (i, 0, 0)),
                pl.BlockSpec((per_shard, BLK, hidden), lambda i, jr: (i, 0, 0)),
                whole_mask,
            ],
            out_specs=(pairs, per_hidden),
            scratch_shapes=[pltpu.VMEM((rows, hidden), F32)],
        ),
        compiler_params=params(40),
    )(j.reshape(1), tk, w1hi, w1lo, relu_mask)

    g_in = grads(tt, dh, m_in, h_in, n_in, at, slots, tok_peers, scale)
    grad_in = sum_over_tok(*g_in)
    g_out = grads(ht, uc, h_out, m_out, n_out, at, slots, tok_peers, scale)
    grad_out = sum_over_tok(*g_out)

    token_grad = terms[1]
    for i in range(sources):
        if i != 1:
            pairs_i = [(s, (s - 1 + i) % peers) for s in range(peers)]
            token_grad = token_grad + lax.ppermute(terms[i], "hid", pairs_i)
    return (token_grad, grad_in, grad_out)


def solution(mesh):
    return jax.shard_map(
        per_device,
        mesh=mesh,
        in_specs=(
            P("tok", "hid"),
            P("tok", "hid"),
            P("tok", "hid"),
            P("hid", None, None),
            P("hid", None, None),
            P("hid", None),
            P("hid", None),
            P("hid", None),
        ),
        out_specs=(P("tok", "hid"), P("hid", "tok", None), P("hid", "tok", None)),
        check_vma=False,
    )
```

```python
import math

import jax
import jax.numpy as jnp
from jax import lax
from jax.experimental import pallas as pl
from jax.experimental.pallas import tpu as pltpu
from jax.sharding import PartitionSpec as P


DB = 32
BLK = 128
SLOTS_A_STEP = 12
SIDE = 4

F32 = jnp.float32
BF16 = jnp.bfloat16


def halves(x):
    hi = x.astype(BF16)
    lo = (x - hi.astype(F32)).astype(BF16)
    return hi, lo


def dot_nn(a, b):
    return lax.dot_general(a, b, (((1,), (0,)), ((), ())), preferred_element_type=F32)


def dot_nt(a, b):
    return lax.dot_general(a, b, (((1,), (1,)), ((), ())), preferred_element_type=F32)


def params(mib):
    return pltpu.CompilerParams(
        dimension_semantics=("arbitrary",), vmem_limit_bytes=mib * 1024 * 1024
    )


def dense_in_kernel(m_ref, h_ref, w_ref, hi_ref, lo_ref):
    step = pl.program_id(0)

    @pl.when(step == 0)
    def _():
        hi_ref[...] = jnp.zeros_like(hi_ref)
        lo_ref[...] = jnp.zeros_like(lo_ref)

    for q in range(SLOTS_A_STEP):
        s = step * SLOTS_A_STEP + q
        hi, lo = halves(w_ref[q])
        col = pl.multiple_of(h_ref[s] * BLK, BLK)
        hi_ref[m_ref[s], :, pl.ds(col, BLK)] = hi
        lo_ref[m_ref[s], :, pl.ds(col, BLK)] = lo


def dense_out_kernel(m_ref, h_ref, w_ref, hi_ref, lo_ref):
    step = pl.program_id(0)

    @pl.when(step == 0)
    def _():
        hi_ref[...] = jnp.zeros_like(hi_ref)
        lo_ref[...] = jnp.zeros_like(lo_ref)

    for q in range(SLOTS_A_STEP):
        s = step * SLOTS_A_STEP + q
        hi, lo = halves(w_ref[q])
        row = pl.multiple_of(h_ref[s] * BLK, BLK)
        col = pl.multiple_of((m_ref[s] % 2) * BLK, BLK)
        hi_ref[m_ref[s] // 2, pl.ds(row, BLK), pl.ds(col, BLK)] = hi
        lo_ref[m_ref[s] // 2, pl.ds(row, BLK), pl.ds(col, BLK)] = lo


def dense(kernel, weight, place, hidden, shape):
    slots = weight.shape[0]
    out = jax.ShapeDtypeStruct(shape, BF16)
    whole = pl.BlockSpec(shape, lambda i, *_: (0, 0, 0))
    return pl.pallas_call(
        kernel,
        out_shape=(out, out),
        grid_spec=pltpu.PrefetchScalarGridSpec(
            num_scalar_prefetch=2,
            grid=(slots // SLOTS_A_STEP,),
            in_specs=[pl.BlockSpec((SLOTS_A_STEP, BLK, BLK), lambda i, *_: (i, 0, 0))],
            out_specs=(whole, whole),
        ),
        compiler_params=params(50),
    )(place, hidden, weight)


def add_up(acc, part):
    step = pl.program_id(0)

    @pl.when(step == 0)
    def _():
        acc[...] = part

    @pl.when(step > 0)
    def _():
        acc[...] += part


def back_part(u_ref, whi_ref, wlo_ref, uc_ref):
    hi, lo = halves(u_ref[0])
    for b in range(2):
        uc_ref[b, :, :BLK] = hi[:, b * BLK : (b + 1) * BLK]
        uc_ref[b, :, BLK:] = lo[:, b * BLK : (b + 1) * BLK]
    return dot_nt(hi, whi_ref[0]) + dot_nt(hi, wlo_ref[0]) + dot_nt(lo, whi_ref[0])


def back_early_kernel(u_ref, whi_ref, wlo_ref, uc_ref, acc_ref):
    add_up(acc_ref, back_part(u_ref, whi_ref, wlo_ref, uc_ref))


def back_late_kernel(
    u_ref, whi_ref, wlo_ref, early_ref, mask_ref, _, uc_ref, dhi_ref, dlo_ref, dh_ref, acc
):
    add_up(acc, back_part(u_ref, whi_ref, wlo_ref, uc_ref))

    @pl.when(pl.program_id(0) == pl.num_programs(0) - 1)
    def _():
        d = (acc[...] + early_ref[...]) * mask_ref[...].astype(F32)
        dhi, dlo = halves(d)
        dhi_ref[...] = dhi
        dlo_ref[...] = dlo
        for h in range(dh_ref.shape[0]):
            dh_ref[h, :, :BLK] = dhi[:, h * BLK : (h + 1) * BLK]
            dh_ref[h, :, BLK:] = dlo[:, h * BLK : (h + 1) * BLK]


def terms_kernel(dhi_ref, dlo_ref, whi_ref, wlo_ref, out_ref):
    hidden = dhi_ref.shape[1]
    whi = whi_ref[...].reshape(2 * BLK, hidden)
    wlo = wlo_ref[...].reshape(2 * BLK, hidden)
    hi = dhi_ref[...]
    out_ref[0] = dot_nt(hi, whi) + dot_nt(hi, wlo) + dot_nt(dlo_ref[...], whi)


def pre_part(t_ref, whi_ref, wlo_ref, tt_ref):
    hidden = whi_ref.shape[2]
    t = t_ref[0]
    hi, lo = halves(t)
    whi = whi_ref[...].reshape(2 * BLK, hidden)
    wlo = wlo_ref[...].reshape(2 * BLK, hidden)
    for b in range(2):
        thi, tlo = halves(t[:, b * BLK : (b + 1) * BLK].T)
        tt_ref[b, :BLK, :] = thi
        tt_ref[b, BLK:, :] = tlo
    return dot_nn(hi, whi) + dot_nn(hi, wlo) + dot_nn(lo, whi)


def pre_early_kernel(t_ref, whi_ref, wlo_ref, tt_ref, acc_ref):
    add_up(acc_ref, pre_part(t_ref, whi_ref, wlo_ref, tt_ref))


def pre_late_kernel(t_ref, whi_ref, wlo_ref, early_ref, mask_ref, _, tt_ref, ht_ref, acc):
    add_up(acc, pre_part(t_ref, whi_ref, wlo_ref, tt_ref))

    @pl.when(pl.program_id(0) == pl.num_programs(0) - 1)
    def _():
        hid = (acc[...] + early_ref[...]) * mask_ref[...].astype(F32)
        for h in range(ht_ref.shape[0]):
            hhi, hlo = halves(hid[:, h * BLK : (h + 1) * BLK].T)
            ht_ref[h, :BLK, :] = hhi
            ht_ref[h, BLK:, :] = hlo


def grad_kernel(scale, a_ref, b_ref, n_ref, at_ref, left_ref, right_ref, mine_ref, other_ref, buf):
    step = pl.program_id(0)
    hops, _, rows, _ = mine_ref.shape
    for q in range(SLOTS_A_STEP):
        s = step * SLOTS_A_STEP + q
        r = dot_nn(left_ref[a_ref[s]], right_ref[b_ref[s]])
        g = (r[:BLK, :BLK] + (r[:BLK, BLK:] + r[BLK:, :BLK] + r[BLK:, BLK:])) * scale
        buf[q] = jnp.where(s < n_ref[0], g, 0.0)
        for k in range(hops):
            mine_ref[k, q] = buf[q, pl.ds(pl.multiple_of(at_ref[k], rows), rows), :]
            other_ref[k, q] = buf[q, pl.ds(pl.multiple_of(at_ref[hops + k], rows), rows), :]


def grads(left, right, a, b, count, at, slots, peers, scale):
    rows = BLK // peers
    hops = peers // 2
    out = jax.ShapeDtypeStruct((hops, slots, rows, BLK), F32)
    out_spec = pl.BlockSpec((hops, SLOTS_A_STEP, rows, BLK), lambda i, *_: (0, i, 0, 0))
    return pl.pallas_call(
        lambda *refs: grad_kernel(scale, *refs),
        out_shape=(out, out),
        grid_spec=pltpu.PrefetchScalarGridSpec(
            num_scalar_prefetch=4,
            grid=(slots // SLOTS_A_STEP,),
            in_specs=[
                pl.BlockSpec(left.shape, lambda i, *_: (0, 0, 0)),
                pl.BlockSpec(right.shape, lambda i, *_: (0, 0, 0)),
            ],
            out_specs=(out_spec, out_spec),
            scratch_shapes=[pltpu.VMEM((SLOTS_A_STEP, BLK, BLK), F32)],
        ),
        compiler_params=params(40),
    )(a, b, count, at, left, right)


def from_z(value, k, only_x=None):
    pairs = [
        ((z + k) % SIDE * SIDE + x, z * SIDE + x)
        for z in range(SIDE)
        for x in range(SIDE)
        if only_x is None or x == only_x
    ]
    return lax.ppermute(value, "hid", pairs)


def from_x(value, k):
    pairs = [
        (z * SIDE + (x + k) % SIDE, z * SIDE + x) for z in range(SIDE) for x in range(SIDE)
    ]
    return lax.ppermute(value, "hid", pairs)


def from_y(value, k):
    pairs = [((y + k) % SIDE * 2 + c, y * 2 + c) for y in range(SIDE) for c in range(2)]
    return lax.ppermute(value, "tok", pairs)


def from_core(value):
    return lax.ppermute(value, "tok", [(i, i ^ 1) for i in range(2 * SIDE)])


def pick(value, start, count):
    return lax.dynamic_slice_in_dim(value, start.astype(jnp.int32), count, 0)


EARLY = (0, 1, 2, 4, 5, 6, 8, 9)
LATE = (3, 7)


def band_z_first(own, x):
    next1 = from_z(own, 1)
    next2, before = from_z(own, 2), from_z(own, -1, SIDE - 1)
    column = jnp.stack([before, own, next1, next2])
    right = from_x(pick(column, 1 + (x == 0), 2), 1)
    left = from_x(pick(column, 1 - (x == SIDE - 1), 3), -1)
    far0 = from_x(jnp.where(x == 0, right[1], right[0]), 1)
    far1 = from_x(jnp.where(x == SIDE - 1, left[1], left[2]), -1)
    early = [left[0], own, right[0], left[1], next1, right[1], left[2], next2]
    return jnp.stack(early), jnp.stack([far0, far1])


def band_x_first(own, x):
    row = [own, from_x(own, 1), from_x(own, 2), from_x(own, -1)]
    above = from_z(jnp.stack(row), 1)
    below = from_z(jnp.stack(row[2:]), -1)
    relayed = from_z(below, -1)
    top = from_z(above[:2], 1)
    above2 = [top[0], top[1], relayed[0], relayed[1]]
    near, far = [], []
    for d in range(1, SIDE):
        wrap = x + d >= SIDE
        near.append(jnp.where(wrap, above[d], row[d]))
        far.append(jnp.where(wrap, above2[d], above[d]))
    before = jnp.where(x == 0, below[1], row[3])
    return jnp.stack([before, own, *near, above[0]]), jnp.stack([*far, above2[0]])


def sum_over_hid(terms, x):
    right = from_x(jnp.stack([terms[2], terms[6]]), -1)
    left = from_x(jnp.stack([terms[0], terms[4], terms[8]]), 1)
    far = from_x(jnp.stack([terms[3], terms[7]]), 2)
    zero = jnp.zeros_like(terms[0])

    def moved(first, values):
        rows = [zero] * first + values
        return rows + [zero] * (SIDE - len(rows))

    own_rows = [zero, terms[1], terms[5], terms[9]]
    right_rows = [
        jnp.where(x == 0, a, b)
        for a, b in zip(moved(2, [right[0], right[1]]), moved(1, [right[0], right[1]]))
    ]
    far_rows = [
        jnp.where(x < 2, a, b)
        for a, b in zip(moved(2, [far[0], far[1]]), moved(1, [far[0], far[1]]))
    ]
    three = [left[0], left[1], left[2]]
    left_rows = [
        jnp.where(x == SIDE - 1, a, b) for a, b in zip(moved(0, three), moved(1, three))
    ]
    rows = [a + b + c + d for a, b, c, d in zip(own_rows, right_rows, far_rows, left_rows)]
    return rows[1] + from_z(rows[2], -1) + from_z(rows[3], -2) + from_z(rows[0], 1, SIDE - 1)


def sum_over_tok(mine, other):
    part = mine + from_core(other)
    half = part.shape[1] // 2
    up = from_y(part[2, :half], -1)
    down = from_y(part[2, half:], 1)
    to_up = jnp.concatenate([part[1, :half] + up, part[1, half:]])
    to_down = jnp.concatenate([part[3, :half], part[3, half:] + down])
    return part[0] + from_y(to_up, -1) + from_y(to_down, 1)


def per_device(tokens, upstream, relu_mask, weight_in, weight_out, kept_in, kept_out, kept_count):
    tok_peers = lax.axis_size("tok")
    j = lax.axis_index("hid").astype(jnp.int32)
    rows, width = tokens.shape
    hidden = relu_mask.shape[1]
    hidden_count = hidden // BLK
    slots = weight_in.shape[0]
    per_shard = width // BLK
    sources = 10
    band = sources * per_shard
    scale = 1.0 / math.sqrt(rows * tok_peers)
    first = (j - 1) * per_shard
    live = jnp.arange(slots, dtype=jnp.int32)
    m_in = (kept_in[:, 0] - first) % DB
    m_in = jnp.where(m_in < band, m_in, 0)
    h_in = jnp.clip(kept_in[:, 1], 0, hidden_count - 1)
    h_out = jnp.clip(kept_out[:, 0], 0, hidden_count - 1)
    m_out = (kept_out[:, 1] - first) % DB
    m_out = jnp.where(m_out < band, m_out, 0)
    source = m_out // per_shard
    place = jnp.zeros_like(source)
    for at_place, k in enumerate(EARLY + LATE):
        place = place + jnp.where(source == k, at_place, 0)
    m_out = place * per_shard + m_out % per_shard
    n_in = kept_count[0, 0].reshape(1)
    n_out = kept_count[0, 1].reshape(1)
    put_in = jnp.where(live < n_in, m_in, band)
    put_out = jnp.where(live < n_out, m_out, band)

    x = j % SIDE
    up_early, up_late = band_z_first(upstream, x)
    tk_early, tk_late = band_x_first(tokens, x)
    t = lax.axis_index("tok").astype(jnp.int32)
    hop = jnp.arange(SIDE, dtype=jnp.int32)
    column = (t // 2 + hop) % SIDE * 2
    at = jnp.concatenate([column + t % 2, column + 1 - t % 2]) * (BLK // tok_peers)

    w2hi, w2lo = dense(dense_out_kernel, weight_out, put_out, h_out, (sources + 1, hidden, width))
    w1hi, w1lo = dense(dense_in_kernel, weight_in, put_in, h_in, (band + per_shard, BLK, hidden))

    def two_calls(early_kernel, late_kernel, early, late, whi, wlo, w_block, late_outs, late_specs):
        n_early, n_late = early.shape[0], late.shape[0]
        unit = pl.BlockSpec((1, rows, width), lambda i: (i, 0, 0))
        flat = pl.BlockSpec((rows, hidden), lambda i: (0, 0))
        blocks = jax.ShapeDtypeStruct((band, rows, width), BF16)
        packed, acc = pl.pallas_call(
            early_kernel,
            out_shape=(blocks, jax.ShapeDtypeStruct((rows, hidden), F32)),
            grid=(n_early,),
            in_specs=[unit] + [pl.BlockSpec(w_block, lambda i: (i, 0, 0))] * 2,
            out_specs=(pl.BlockSpec((per_shard, rows, width), lambda i: (i, 0, 0)), flat),
            compiler_params=params(40),
        )(early, whi, wlo)
        return pl.pallas_call(
            late_kernel,
            out_shape=(blocks, *late_outs),
            grid=(n_late,),
            in_specs=[unit]
            + [pl.BlockSpec(w_block, lambda i: (i + n_early, 0, 0))] * 2
            + [flat, flat, pl.BlockSpec(memory_space=pl.ANY)],
            out_specs=(
                pl.BlockSpec((per_shard, rows, width), lambda i: (i + n_early, 0, 0)),
                *late_specs,
            ),
            scratch_shapes=[pltpu.VMEM((rows, hidden), F32)],
            input_output_aliases={5: 0},
            compiler_params=params(40),
        )(late, whi, wlo, acc, relu_mask, packed)

    flat_out = jax.ShapeDtypeStruct((rows, hidden), BF16)
    split_out = jax.ShapeDtypeStruct((hidden_count, rows, width), BF16)
    flat_spec = pl.BlockSpec((rows, hidden), lambda i: (0, 0))
    split_spec = pl.BlockSpec((hidden_count, rows, width), lambda i: (0, 0, 0))
    uc, dhi, dlo, dh = two_calls(
        back_early_kernel,
        back_late_kernel,
        up_early,
        up_late,
        w2hi,
        w2lo,
        (1, hidden, width),
        (flat_out, flat_out, split_out),
        (flat_spec, flat_spec, split_spec),
    )

    terms = pl.pallas_call(
        terms_kernel,
        out_shape=jax.ShapeDtypeStruct((sources, rows, width), F32),
        grid=(sources,),
        in_specs=[
            pl.BlockSpec((rows, hidden), lambda i: (0, 0)),
            pl.BlockSpec((rows, hidden), lambda i: (0, 0)),
            pl.BlockSpec((per_shard, BLK, hidden), lambda i: (i, 0, 0)),
            pl.BlockSpec((per_shard, BLK, hidden), lambda i: (i, 0, 0)),
        ],
        out_specs=pl.BlockSpec((1, rows, width), lambda i: (i, 0, 0)),
        compiler_params=params(40),
    )(dhi, dlo, w1hi, w1lo)
    terms, tk_late = lax.optimization_barrier((terms, tk_late))

    tt, ht = two_calls(
        pre_early_kernel,
        pre_late_kernel,
        tk_early,
        tk_late,
        w1hi,
        w1lo,
        (per_shard, BLK, hidden),
        (split_out,),
        (split_spec,),
    )

    g_in = grads(tt, dh, m_in, h_in, n_in, at, slots, tok_peers, scale)
    grad_in = sum_over_tok(*g_in)
    g_out = grads(ht, uc, h_out, m_out, n_out, at, slots, tok_peers, scale)
    grad_out = sum_over_tok(*g_out)

    token_grad = sum_over_hid(terms, x)
    return (token_grad, grad_in, grad_out)


def solution(mesh):
    return jax.shard_map(
        per_device,
        mesh=mesh,
        in_specs=(
            P("tok", "hid"),
            P("tok", "hid"),
            P("tok", "hid"),
            P("hid", None, None),
            P("hid", None, None),
            P("hid", None),
            P("hid", None),
            P("hid", None),
        ),
        out_specs=(P("tok", "hid"), P("hid", "tok", None), P("hid", "tok", None)),
        check_vma=False,
    )
```
